32 devices in a mesh: groups: 2 (over y), cluster: 4 (over x, core), station: 4 (over z).
Axes of the slice: x: 2, y: 2, z: 4, core: 2. Of those that a mesh axis runs over, the one named last changes fastest.
Arguments:
- waveforms: float32 [256, 16, 3, 256], P(('groups', 'cluster'), 'station'), parts along dimension 0, may hold values from -120 to 120
- event_mask: int32 [256, 16], P(('groups', 'cluster'), 'station'), parts along dimension 0, may hold values 0 or 1
- station_weight: float32 [32], P('groups'), parts along dimension 0, may hold values from 0.01 to 10
- partners: int32 [4, 8], P(None, 'groups'), parts along dimension 1, may hold values from 0 to 3, as said below
- pair_list: int32 [4, 8, 256, 2], P(None, ('groups', 'cluster')), parts along dimension 1, may hold values from 0 to 31
- counts: int32 [8], P('groups'), parts along dimension 0, may hold values from 16 to 32, as said below
Outputs:
- stacked: float32 [4, 8, 256, 512], P(None, ('groups', 'cluster'), 'station'), parts along dimension 1
The draws below stay inside these ranges and needn't reach their ends.
There are 2 independent parts, one for each index of `groups`. The reference program is written for one: setup_inputs(seed, part) draws one part's arguments, and reference() takes and returns one part's arrays. A program takes and returns all parts, laid end to end along the dimension named above; each array names one. Nothing has to cross between parts.
Inputs may be any that keep to these rules, and one draw needn't show every extreme that they name: `partners`: in every round each cluster is paired with itself or with one of its two neighbours on the cluster cycle (index plus or minus one, modulo 4), and the pairing is mutual. `counts`: event slots of a cluster at or above its count are padding. Every draw has a cluster holding 32 events and another holding 32 // 2.
All inputs are finite; a program needn't handle non-finite values. No bound on the sum of `event_mask` on one device may be relied on, other than what follows from the above.
Results may differ from the reference program's by a relative error of at most 0.0003.
Values sent between devices are 32-bit elements; how exact they have to be, the bound alone decides.
A program may use at most 64 MiB of HBM per device.

```python
import math
import jax
import jax.numpy as jnp
from jax import lax

E_DEV = 32
CH = 3
NT = 256
ROUNDS = 4
PAIRS = 256
NCL = 4
NEV = 128
NST = 16


def draw_waveforms(key, part):
    subkeys = jax.random.split(key, 5)
    wavelet = jax.random.truncated_normal(subkeys[0], -4.0, 4.0, (NST, CH, NT), jnp.float32)
    delays = jax.random.randint(subkeys[1], (NEV,), 0, 32)
    positions = (jnp.arange(NT, dtype=jnp.int32)[None, :] - delays[:, None]) % NT
    delayed_seismograms = jnp.transpose(jnp.take(wavelet, positions, axis=2), (2, 0, 1, 3))
    spread = jax.random.truncated_normal(subkeys[2], -4.0, 4.0, (NEV, NST, CH, NT), jnp.float32)
    noise_level = jnp.exp(jax.random.uniform(subkeys[3], (NEV, NST), jnp.float32, math.log(0.3), math.log(2.0)))
    amplitude = jnp.exp(jax.random.uniform(subkeys[4], (NEV, NST), jnp.float32, math.log(0.1), math.log(10.0)))
    traces = amplitude[:, :, None, None] * (delayed_seismograms + noise_level[:, :, None, None] * spread)
    return traces.astype(jnp.float32)


def draw_partners(key, part):
    subkeys = jax.random.split(key, 2)
    matching_kind = jax.random.randint(subkeys[0], (ROUNDS, 1), 0, 2)
    keep_edge = jax.random.randint(subkeys[1], (ROUNDS, NCL), 0, 2)
    cluster_ids = jnp.arange(NCL, dtype=jnp.int32)[None, :]
    starts_edge = (cluster_ids + matching_kind) % 2 == 0
    edge_start = jnp.where(starts_edge, cluster_ids, (cluster_ids - 1) % NCL)
    kept = jnp.take_along_axis(keep_edge, jnp.broadcast_to(edge_start, (ROUNDS, NCL)).astype(jnp.int32), axis=1)
    direction = jnp.where(starts_edge, 1, -1)
    neighbour = (cluster_ids + direction) % NCL
    return jnp.where(kept == 1, neighbour, cluster_ids).astype(jnp.int32)


def draw_counts(key, part):
    subkeys = jax.random.split(key, 3)
    counts = jax.random.randint(subkeys[0], (NCL,), E_DEV // 2, E_DEV + 1)
    full_cluster = jax.random.randint(subkeys[1], (), 0, NCL)
    half_cluster = (full_cluster + jax.random.randint(subkeys[2], (), 1, NCL)) % NCL
    cluster_ids = jnp.arange(NCL, dtype=jnp.int32)
    counts = jnp.where(cluster_ids == full_cluster, E_DEV, counts)
    counts = jnp.where(cluster_ids == half_cluster, E_DEV // 2, counts)
    return counts.astype(jnp.int32)


def place_ends(drawn, rng, low, high):
    spot = [jax.random.randint(jax.random.fold_in(rng, axis), (), 0, length) for axis, length in enumerate(drawn.shape)]
    widest = drawn.shape.index(max(drawn.shape))
    beside = spot[:widest] + [(spot[widest] + 1) % drawn.shape[widest]] + spot[widest + 1:]
    return drawn.at[tuple(spot)].set(low).at[tuple(beside)].set(high)


def setup_inputs(seed: int = 0, part: int = 0) -> dict:
    splits = jax.random.split(jax.random.key(seed), 7)
    own_keys = jax.random.split(jax.random.fold_in(splits[6], part), 7)
    return {
        "waveforms": draw_waveforms(jax.random.fold_in(jax.random.fold_in(splits[6], part), 71), part),
        "event_mask": place_ends((jax.random.randint(own_keys[1], (NEV, NST), 0, 4) < 3).astype(jnp.int32), jax.random.fold_in(own_keys[1], 1), 0, 1),
        "station_weight": jnp.clip(jnp.exp(jax.random.uniform(own_keys[2], (NST,), jnp.float32, math.log(0.01), math.log(10.0))), 0.01, 10.0),
        "partners": draw_partners(jax.random.fold_in(jax.random.fold_in(splits[6], part), 71), part),
        "pair_list": place_ends(jax.random.randint(own_keys[4], (ROUNDS, NCL, PAIRS, 2), 0, E_DEV), jax.random.fold_in(own_keys[4], 1), 0, E_DEV - 1).astype(jnp.int32),
        "counts": draw_counts(jax.random.fold_in(jax.random.fold_in(splits[6], part), 71), part),
    }


epsilon = 1e-06
HIGHEST = lax.Precision.HIGHEST

def make_tables(seismogram_readings):
    record_duration = 2 * seismogram_readings
    time_points = jnp.arange(seismogram_readings, dtype=jnp.int32)
    rotation_radians = time_points[:, None] * time_points[None, :] % record_duration
    angles = rotation_radians.astype(jnp.float32) * (math.pi / seismogram_readings)
    forward = jnp.concatenate([jnp.cos(angles), -jnp.sin(angles)], axis=1)
    column = jnp.arange(record_duration, dtype=jnp.int32)
    delayed_seismograms = (column + seismogram_readings) % record_duration
    backward_rotation_radians = time_points[:, None] * delayed_seismograms[None, :] % record_duration
    angles_back = backward_rotation_radians.astype(jnp.float32) * (math.pi / seismogram_readings)
    normalizing_multiplier = jnp.where(time_points == 0, 1.0, 2.0).astype(jnp.float32)[:, None] / record_duration
    inverse = jnp.concatenate([normalizing_multiplier * jnp.cos(angles_back), -normalizing_multiplier * jnp.sin(angles_back)], axis=0)
    return (forward, inverse)

def normalized(waveforms, event_mask):
    energy = lax.optimization_barrier(jnp.sum(waveforms * waveforms, axis=-1, keepdims=True))
    scaled = waveforms * lax.rsqrt(energy + epsilon)
    return scaled * event_mask[:, :, None, None].astype(jnp.float32)

def transform(traces, forward):
    events, stations, channels, seismogram_readings = traces.shape
    flattened = traces.reshape(events * stations * channels, seismogram_readings)
    spectra = jnp.dot(flattened, forward, precision=HIGHEST, preferred_element_type=jnp.float32)
    return spectra.reshape(events, stations * channels, 2 * seismogram_readings)

def cross_block(own_side, other_side, first_index, second):
    half_width = own_side.shape[-1] // 2
    left_rows = jnp.take(own_side, first_index, axis=0)
    right_rows = jnp.take(other_side, second, axis=0)
    real_part = lax.optimization_barrier(jnp.sum(left_rows[..., :half_width] * right_rows[..., :half_width] + left_rows[..., half_width:] * right_rows[..., half_width:], axis=1))
    imag_part = lax.optimization_barrier(jnp.sum(left_rows[..., half_width:] * right_rows[..., :half_width] - left_rows[..., :half_width] * right_rows[..., half_width:], axis=1))
    return jnp.concatenate([real_part, imag_part], axis=-1)

def pair_spectra(own_side, other_side, pairs_now, valid_pairs):
    pair_count = pairs_now.shape[0]
    block_rows = math.gcd(pair_count, 64)
    firsts = pairs_now[:, 0].reshape(pair_count // block_rows, block_rows)
    seconds = pairs_now[:, 1].reshape(pair_count // block_rows, block_rows)

    def one_block(indices):
        return cross_block(own_side, other_side, indices[0], indices[1])
    stacked_rows = lax.map(one_block, (firsts, seconds)).reshape(pair_count, own_side.shape[-1])
    return stacked_rows * valid_pairs[:, None]

def reference(waveforms, event_mask, station_weight, partners, pair_list, counts):
    forward, inverse = make_tables(NT)
    blocks = waveforms.reshape(NCL, E_DEV, NST, CH, NT)
    mask_blocks = event_mask.reshape(NCL, E_DEV, NST)

    def spectra_of(inputs):
        return transform(normalized(inputs[0], inputs[1]), forward)
    all_spectra = lax.map(spectra_of, (blocks, mask_blocks))
    weight_rows = jnp.repeat(station_weight, CH)
    network_scale = 1.0 / (CH * jnp.sum(station_weight))
    results = []
    for turn_index in range(ROUNDS):

        def one_cluster(cluster_id):
            partner_now = partners[turn_index, cluster_id]
            own_side = all_spectra[cluster_id] * weight_rows[None, :, None]
            other_side = all_spectra[partner_now]
            pairs_now = pair_list[turn_index, cluster_id]
            valid_pairs = ((pairs_now[:, 0] < counts[cluster_id]) & (pairs_now[:, 1] < counts[partner_now])).astype(jnp.float32)
            cross = pair_spectra(own_side, other_side, pairs_now, valid_pairs)
            return jnp.dot(cross, inverse, precision=HIGHEST, preferred_element_type=jnp.float32) * network_scale
        results.append(lax.map(one_cluster, jnp.arange(NCL, dtype=jnp.int32)))
    return jnp.stack(results)
```

```python
import functools
import math

import jax
import jax.numpy as jnp
import numpy as np
from jax import lax
from jax.experimental import pallas as pl
from jax.experimental.pallas import tpu as pltpu
from jax.sharding import PartitionSpec as P

epsilon = 1e-06
LANES = 128
MESH = pl.DeviceIdType.MESH


def split_table(table):
    high = table.astype(np.float32).astype(jnp.bfloat16)
    low = (table - high.astype(np.float64)).astype(np.float32).astype(jnp.bfloat16)
    return np.asarray(high), np.asarray(low)


def make_tables(samples):
    duration = 2 * samples
    time_points = np.arange(samples)
    angles = (time_points[:, None] * time_points[None, :] % duration) * (math.pi / samples)
    forward = np.concatenate([np.cos(angles), -np.sin(angles)], axis=1)
    lags = (np.arange(duration) + samples) % duration
    back = (time_points[:, None] * lags[None, :] % duration) * (math.pi / samples)
    scale = np.where(time_points == 0, 1.0, 2.0)[:, None] / duration
    inverse = np.concatenate([scale * np.cos(back), -scale * np.sin(back)], axis=0)
    return split_table(forward) + split_table(inverse)


def halves(x):
    high = x.astype(jnp.bfloat16)
    return high, (x - high.astype(jnp.float32)).astype(jnp.bfloat16)


def dot3(x, table_high, table_low):
    high, low = halves(x)
    dot = functools.partial(jnp.dot, preferred_element_type=jnp.float32)
    return dot(high, table_high) + (dot(high, table_low) + dot(low, table_high))


def kernel(sizes, first_ref, second_ref, weight_ref, traces_ref, scale_ref, fh_ref, fl_ref, gh_ref,
           gl_ref, out_ref, arrived, weighted, spectra, part, from_below, from_above,
           side_send, side_recv, up_send, up_recv, down_send, down_recv):
    events, rows, rounds, chain, share, ring, channels = sizes
    cols = fh_ref.shape[1] // LANES
    half = cols // 2
    lines = rows * cols
    cluster = lax.axis_index("cluster")
    here = lax.axis_index("station")
    right, left = lax.rem(cluster + 1, ring), lax.rem(cluster + ring - 1, ring)

    barrier = pltpu.get_barrier_semaphore()
    for side in (left, right):
        pl.semaphore_signal(barrier, inc=1, device_id={"cluster": side}, device_id_type=MESH)

    @pl.when(here > 0)
    def _():
        pl.semaphore_signal(barrier, inc=1, device_id={"station": here - 1}, device_id_type=MESH)

    @pl.when(here < chain - 1)
    def _():
        pl.semaphore_signal(barrier, inc=1, device_id={"station": here + 1}, device_id_type=MESH)

    pl.semaphore_wait(barrier, 2 + (here + chain - 1) // chain + (2 * chain - 2 - here) // chain)

    def to_side(slot, side):
        return pltpu.make_async_remote_copy(
            src_ref=traces_ref, dst_ref=arrived.at[slot], send_sem=side_send.at[slot],
            recv_sem=side_recv.at[slot], device_id={"cluster": side}, device_id_type=MESH)

    to_right, to_left = to_side(0, right), to_side(1, left)
    to_right.start()
    to_left.start()

    def place(values, row, base, ref):
        for col in range(cols):
            line = (col // half) * (lines // 2) + row * half + col % half
            start = base * lines + line
            flat = ref.reshape(ref.shape[0] * lines, LANES)
            flat[pl.ds(start, events, stride=lines), :] = values[:, col * LANES:(col + 1) * LANES]

    def transform(source, base, also_weighted):
        group = 4 if rows % 4 == 0 else 1
        for first in range(0, rows, group):
            found = dot3(source[pl.ds(first * events, group * events), :], fh_ref[...], fl_ref[...])
            for k in range(group):
                row = first + k
                values = found[k * events:(k + 1) * events]
                place(values, row, base * events, spectra)
                if also_weighted:
                    place(values * weight_ref[here * (rows // channels) + row // channels], row, 0, weighted)

    transform(traces_ref, 0, True)
    to_left.wait()
    transform(arrived.at[1], 2, False)
    to_right.wait()
    transform(arrived.at[0], 1, False)

    sub = lax.broadcasted_iota(jnp.int32, (8, LANES), 0)
    in_low4 = sub < 4
    in_low2 = (sub & 2) == 0

    def fold(x, y, lower, by):
        return jnp.where(lower, x, y) + pltpu.roll(jnp.where(lower, y, x), by, 0)

    deep = lines // 2

    def one_pair(spot):
        a = weighted[first_ref[spot]]
        b = spectra[second_ref[spot]]
        re_a, im_a, re_b, im_b = a[:deep], a[deep:], b[:deep], b[deep:]
        real = re_a * re_b + im_a * im_b
        imag = im_a * re_b - re_a * im_b
        return (sum(real[k:k + 8] for k in range(0, deep, 8)),
                sum(imag[k:k + 8] for k in range(0, deep, 8)))

    def fill(turn, dest):
        base = (turn * chain + dest) * share

        def body(step, carry):
            for k in range(0, 8, 2):
                spot = base + step * 8 + k
                real0, imag0 = one_pair(spot)
                real1, imag1 = one_pair(spot + 1)
                reals = fold(real0, real1, in_low4, 4)
                imags = fold(imag0, imag1, in_low4, 4)
                both = jnp.where(in_low2, reals, imags) + jnp.where(
                    in_low2, pltpu.roll(reals, 6, 0), pltpu.roll(imags, 2, 0))
                part[turn * chain + dest, pl.ds(pl.multiple_of(step * 32 + k * 4, 8), 8), :] = both
            return carry

        lax.fori_loop(0, share // 8, body, 0)

    def upward(turn, dest):
        spot = turn * chain + dest
        return pltpu.make_async_remote_copy(
            src_ref=part.at[spot], dst_ref=from_below.at[spot], send_sem=up_send.at[spot],
            recv_sem=up_recv.at[spot], device_id={"station": here + 1}, device_id_type=MESH)

    def downward(turn, dest):
        spot = turn * chain + dest
        return pltpu.make_async_remote_copy(
            src_ref=part.at[spot], dst_ref=from_above.at[spot], send_sem=down_send.at[spot],
            recv_sem=down_recv.at[spot], device_id={"station": here - 1}, device_id_type=MESH)

    far_first = sorted(range(chain), key=lambda d: -abs(2 * d - chain + 1))

    def compute(turn):
        for dest in far_first:
            fill(turn, dest)

            @pl.when((here == 0) & (dest > here))
            def _():
                upward(turn, dest).start()

            @pl.when((here == chain - 1) & (dest < here))
            def _():
                downward(turn, dest).start()

    def forward(turn):
        for dest in far_first:
            spot = turn * chain + dest

            @pl.when((here > 0) & (dest > here))
            def _():
                upward(turn, dest).wait_recv()
                part[spot] = part[spot] + from_below[spot]
                upward(turn, dest).start()

            @pl.when((here < chain - 1) & (dest < here))
            def _():
                downward(turn, dest).wait_recv()
                part[spot] = part[spot] + from_above[spot]
                downward(turn, dest).start()

        spot = turn * chain + here

        @pl.when(here > 0)
        def _():
            upward(turn, here).wait_recv()
            part[spot] = part[spot] + from_below[spot]

        @pl.when(here < chain - 1)
        def _():
            downward(turn, here).wait_recv()
            part[spot] = part[spot] + from_above[spot]

        total = jnp.zeros((share, gh_ref.shape[1]), jnp.float32)
        for col in range(cols):
            piece = part[spot, pl.ds(col, share, stride=cols), :]
            table = pl.ds(col * LANES, LANES)
            total = total + dot3(piece, gh_ref[table, :], gl_ref[table, :])
        out_ref[turn] = total * scale_ref[turn]

    compute(0)

    def turn_body(turn, carry):
        compute(turn + 1)
        forward(turn)
        return carry

    lax.fori_loop(0, rounds - 1, turn_body, 0)
    forward(rounds - 1)

    def drain(turn, carry):
        for dest in range(chain):
            @pl.when(dest > here)
            def _():
                upward(turn, dest).wait_send()

            @pl.when(dest < here)
            def _():
                downward(turn, dest).wait_send()
        return carry

    lax.fori_loop(0, rounds, drain, 0)


def on_device(waveforms, event_mask, station_weight, partners, pair_list, counts):
    events, stations, channels, samples = waveforms.shape
    rounds, _, pairs, _ = pair_list.shape
    cluster = lax.axis_index("cluster")
    ring = lax.axis_size("cluster")
    here = lax.axis_index("station")
    chain = lax.axis_size("station")
    rows = stations * channels
    share = pairs // chain
    cols = 2 * samples // LANES
    fh, fl, gh, gl = make_tables(samples)

    energy = jnp.sum(waveforms * waveforms, axis=-1, keepdims=True)
    unit = waveforms * (lax.rsqrt(energy + epsilon) * event_mask[:, :, None, None].astype(jnp.float32))
    traces = jnp.transpose(unit, (1, 2, 0, 3)).reshape(rows * events, samples)

    partner = partners[:, cluster]
    slot = jnp.where(partner == cluster, 0, jnp.where(partner == (cluster + 1) % ring, 2, 1))
    i, j = pair_list[:, 0, :, 0], pair_list[:, 0, :, 1]
    first = i.reshape(-1)
    second = (slot[:, None] * events + j).reshape(-1)
    valid = ((i < counts[cluster]) & (j < counts[partner][:, None])).astype(jnp.float32)
    scale = valid / (channels * jnp.sum(station_weight))
    scale = lax.dynamic_slice_in_dim(scale, here * share, share, 1)[:, :, None]

    vmem = pl.BlockSpec(memory_space=pltpu.VMEM)
    smem = pl.BlockSpec(memory_space=pltpu.SMEM)
    blocks = rounds * chain
    block = pltpu.VMEM((blocks, share * cols, LANES), jnp.float32)
    out = pl.pallas_call(
        functools.partial(kernel, (events, rows, rounds, chain, share, ring, channels)),
        out_shape=jax.ShapeDtypeStruct((rounds, share, 2 * samples), jnp.float32),
        in_specs=[smem, smem, smem] + [vmem] * 6,
        out_specs=vmem,
        scratch_shapes=[
            pltpu.VMEM((2, rows * events, samples), jnp.float32),
            pltpu.VMEM((events, rows * cols, LANES), jnp.float32),
            pltpu.VMEM((3 * events, rows * cols, LANES), jnp.float32),
            block, block, block,
            pltpu.SemaphoreType.DMA((2,)), pltpu.SemaphoreType.DMA((2,)),
            pltpu.SemaphoreType.DMA((blocks,)), pltpu.SemaphoreType.DMA((blocks,)),
            pltpu.SemaphoreType.DMA((blocks,)), pltpu.SemaphoreType.DMA((blocks,)),
        ],
        compiler_params=pltpu.CompilerParams(
            collective_id=0, has_side_effects=True, vmem_limit_bytes=40 << 20),
        name="stack_pairs",
    )(first, second, station_weight, traces, scale, fh, fl, gh, gl)
    return out[:, None]


def solution(mesh):
    return jax.shard_map(
        on_device,
        mesh=mesh,
        in_specs=(
            P(("groups", "cluster"), "station", None, None),
            P(("groups", "cluster"), "station"),
            P("groups"),
            P(None, "groups"),
            P(None, ("groups", "cluster"), None, None),
            P("groups"),
        ),
        out_specs=P(None, ("groups", "cluster"), "station", None),
        check_vma=False,
    )
```

```python
import functools
import math

import jax
import jax.numpy as jnp
import numpy as np
from jax import lax
from jax.experimental import pallas as pl
from jax.experimental.pallas import tpu as pltpu
from jax.sharding import PartitionSpec as P

epsilon = 1e-06
LANES = 128
MESH = pl.DeviceIdType.MESH


def split_table(table):
    high = table.astype(np.float32).astype(jnp.bfloat16)
    low = (table - high.astype(np.float64)).astype(np.float32).astype(jnp.bfloat16)
    return np.asarray(high), np.asarray(low)


def make_tables(samples):
    duration = 2 * samples
    time_points = np.arange(samples)
    angles = (time_points[:, None] * time_points[None, :] % duration) * (math.pi / samples)
    forward = np.concatenate([np.cos(angles), -np.sin(angles)], axis=1)
    lags = (np.arange(duration) + samples) % duration
    back = (time_points[:, None] * lags[None, :] % duration) * (math.pi / samples)
    scale = np.where(time_points == 0, 1.0, 2.0)[:, None] / duration
    inverse = np.concatenate([scale * np.cos(back), -scale * np.sin(back)], axis=0)
    return split_table(forward) + split_table(inverse)


def halves(x):
    high = x.astype(jnp.bfloat16)
    return high, (x - high.astype(jnp.float32)).astype(jnp.bfloat16)


def dot3(x, table_high, table_low):
    high, low = halves(x)
    dot = functools.partial(jnp.dot, preferred_element_type=jnp.float32)
    return dot(high, table_high) + (dot(high, table_low) + dot(low, table_high))


def kernel(sizes, pair_ref, partner_ref, count_ref, weight_ref, traces_ref, fh_hbm, fl_hbm, gh_hbm,
           gl_hbm, out_ref, fh_ref, fl_ref, gh_ref, gl_ref, arrived, end_arrived, weighted,
           spectra, end_weighted, end_spectra, part, from_below, from_above, table_sem, side_send,
           side_recv, end_send, end_recv, up_send, up_recv, down_send, down_recv):
    events, rows, rounds, chain, share, ring, channels = sizes
    cols = fh_ref.shape[1] // LANES
    half = cols // 2
    lines = rows * cols
    cluster = lax.axis_index("cluster")
    here = lax.axis_index("station")
    right, left = lax.rem(cluster + 1, ring), lax.rem(cluster + ring - 1, ring)

    tables = [
        pltpu.make_async_copy(source, target, table_sem.at[k])
        for k, (source, target) in enumerate(
            ((fh_hbm, fh_ref), (fl_hbm, fl_ref), (gh_hbm, gh_ref), (gl_hbm, gl_ref)))
    ]
    for table in tables:
        table.start()

    barrier = pltpu.get_barrier_semaphore()
    for side in (left, right):
        pl.semaphore_signal(barrier, inc=1, device_id={"cluster": side}, device_id_type=MESH)

    @pl.when(here > 0)
    def _():
        pl.semaphore_signal(barrier, inc=1, device_id={"station": here - 1}, device_id_type=MESH)

    @pl.when(here < chain - 1)
    def _():
        pl.semaphore_signal(barrier, inc=1, device_id={"station": here + 1}, device_id_type=MESH)

    pl.semaphore_wait(barrier, 2 + (here + chain - 1) // chain + (2 * chain - 2 - here) // chain)

    def to_side(slot, side):
        return pltpu.make_async_remote_copy(
            src_ref=traces_ref, dst_ref=arrived.at[slot], send_sem=side_send.at[slot],
            recv_sem=side_recv.at[slot], device_id={"cluster": side}, device_id_type=MESH)

    to_right, to_left = to_side(0, right), to_side(1, left)
    to_right.start()
    to_left.start()

    ends = chain >= 4
    pitch = chain - 1 if ends else 1
    at_end = (here == 0) | (here == chain - 1)
    inner = (here == 1) | (here == chain - 2)
    inward = 1 + (here // pitch) * (chain - 3) if ends else here

    def end_copy(k, source, where):
        return pltpu.make_async_remote_copy(
            src_ref=source, dst_ref=end_arrived.at[k], send_sem=end_send.at[k],
            recv_sem=end_recv.at[k], device_id=where, device_id_type=MESH)

    to_inner = end_copy(0, traces_ref, {"station": inward})
    pass_right = end_copy(1, end_arrived.at[0], {"cluster": right})
    pass_left = end_copy(2, end_arrived.at[0], {"cluster": left})

    if ends:
        @pl.when(at_end)
        def _():
            to_inner.start()

    def place(values, row, base, ref):
        for col in range(cols):
            line = (col // half) * (lines // 2) + row * half + col % half
            start = base * lines + line
            flat = ref.reshape(ref.shape[0] * lines, LANES)
            flat[pl.ds(start, events, stride=lines), :] = values[:, col * LANES:(col + 1) * LANES]

    def transform(source, slot, spectra_to, weighted_to, station):
        group = 4 if rows % 4 == 0 else 1
        for first in range(0, rows, group):
            found = dot3(source[pl.ds(first * events, group * events), :], fh_ref[...], fl_ref[...])
            for k in range(group):
                row = first + k
                values = found[k * events:(k + 1) * events]
                place(values, row, slot * events, spectra_to)
                if weighted_to is not None:
                    weight = weight_ref[station * (rows // channels) + row // channels]
                    place(values * weight, row, 0, weighted_to)

    spectra[3 * events] = jnp.zeros(spectra.shape[1:], jnp.float32)
    end_spectra[3 * events] = jnp.zeros(spectra.shape[1:], jnp.float32)
    tables[0].wait()
    tables[1].wait()
    transform(traces_ref, 0, spectra, weighted, here)
    to_left.wait()
    transform(arrived.at[1], 2, spectra, None, here)
    to_right.wait()
    if ends:
        @pl.when(inner)
        def _():
            to_inner.wait_recv()
            pass_right.start()
            pass_left.start()

    transform(arrived.at[0], 1, spectra, None, here)
    tables[2].wait()
    tables[3].wait()

    sub = lax.broadcasted_iota(jnp.int32, (8, LANES), 0)
    in_low4 = sub < 4
    in_low2 = (sub & 2) == 0

    def fold(x, y, lower, by):
        return jnp.where(lower, x, y) + pltpu.roll(jnp.where(lower, y, x), by, 0)

    deep = lines // 2

    def one_pair(spot, turn_facts, left_rows, right_rows):
        slot, own_count, other_count = turn_facts
        first, second = pair_ref[2 * spot], pair_ref[2 * spot + 1]
        valid = (first < own_count) & (second < other_count)
        a = left_rows[first]
        b = right_rows[jnp.where(valid, slot * events + second, 3 * events)]
        re_a, im_a, re_b, im_b = a[:deep], a[deep:], b[:deep], b[deep:]
        real = re_a * re_b + im_a * im_b
        imag = im_a * re_b - re_a * im_b
        return (sum(real[k:k + 8] for k in range(0, deep, 8)),
                sum(imag[k:k + 8] for k in range(0, deep, 8)))

    def fill(turn, dest, left_rows, right_rows, add):
        base = (turn * chain + dest) * share
        partner = partner_ref[turn * ring + cluster]
        slot = jnp.where(partner == cluster, 0, jnp.where(partner == right, 2, 1))
        turn_facts = (slot, count_ref[cluster], count_ref[partner])

        def body(step, carry):
            for k in range(0, 8, 2):
                spot = base + step * 8 + k
                real0, imag0 = one_pair(spot, turn_facts, left_rows, right_rows)
                real1, imag1 = one_pair(spot + 1, turn_facts, left_rows, right_rows)
                reals = fold(real0, real1, in_low4, 4)
                imags = fold(imag0, imag1, in_low4, 4)
                both = jnp.where(in_low2, reals, imags) + jnp.where(
                    in_low2, pltpu.roll(reals, 6, 0), pltpu.roll(imags, 2, 0))
                place_at = pl.ds(pl.multiple_of(step * 32 + k * 4, 8), 8)
                if add:
                    both = both + part[turn * chain + dest, place_at, :]
                part[turn * chain + dest, place_at, :] = both
            return carry

        lax.fori_loop(0, share // 8, body, 0)

    def upward(turn, dest):
        spot = turn * chain + dest
        return pltpu.make_async_remote_copy(
            src_ref=part.at[spot], dst_ref=from_below.at[spot], send_sem=up_send.at[spot],
            recv_sem=up_recv.at[spot], device_id={"station": here + 1}, device_id_type=MESH)

    def downward(turn, dest):
        spot = turn * chain + dest
        return pltpu.make_async_remote_copy(
            src_ref=part.at[spot], dst_ref=from_above.at[spot], send_sem=down_send.at[spot],
            recv_sem=down_recv.at[spot], device_id={"station": here - 1}, device_id_type=MESH)

    far_first = sorted(range(chain), key=lambda d: -abs(2 * d - chain + 1))

    def by_end(low, dest):
        if not ends:
            return False
        return dest == 1 if low else dest == chain - 2

    def compute(turn):
        for dest in far_first:
            given = ((here == 0) & by_end(True, dest)) | ((here == chain - 1) & by_end(False, dest))

            @pl.when(jnp.logical_not(given))
            def _():
                fill(turn, dest, weighted, spectra, False)

            if not by_end(True, dest):
                @pl.when((here == 0) & (dest > here))
                def _():
                    upward(turn, dest).start()

            if not by_end(False, dest):
                @pl.when((here == chain - 1) & (dest < here))
                def _():
                    downward(turn, dest).start()

    def pass_up(turn):
        for dest in far_first:
            spot = turn * chain + dest

            @pl.when((here > 0) & (dest > here))
            def _():
                upward(turn, dest).wait_recv()
                part[spot] = part[spot] + from_below[spot]
                upward(turn, dest).start()

    def pass_down(turn):
        for dest in far_first:
            spot = turn * chain + dest

            @pl.when((here < chain - 1) & (dest < here))
            def _():
                downward(turn, dest).wait_recv()
                part[spot] = part[spot] + from_above[spot]
                downward(turn, dest).start()

    lower = 2 * here < chain

    def pass_near(turn):
        @pl.when(lower)
        def _():
            pass_up(turn)

        @pl.when(jnp.logical_not(lower))
        def _():
            pass_down(turn)

    def pass_far(turn):
        @pl.when(lower)
        def _():
            pass_down(turn)

        @pl.when(jnp.logical_not(lower))
        def _():
            pass_up(turn)

    gets_below = (here > 1) if ends else (here > 0)
    gets_above = (here < chain - 2) if ends else (here < chain - 1)
    weight_sum = weight_ref[0]
    for k in range(1, weight_ref.shape[0]):
        weight_sum = weight_sum + weight_ref[k]
    scale = 1.0 / (channels * jnp.full((1, gh_ref.shape[1]), weight_sum, jnp.float32))

    def final(turn):
        spot = turn * chain + here

        if ends:
            @pl.when(inner)
            def _():
                fill(turn, here, end_weighted, end_spectra, True)

        @pl.when(gets_below)
        def _():
            upward(turn, here).wait_recv()
            part[spot] = part[spot] + from_below[spot]

        @pl.when(gets_above)
        def _():
            downward(turn, here).wait_recv()
            part[spot] = part[spot] + from_above[spot]

        total = jnp.zeros((share, gh_ref.shape[1]), jnp.float32)
        for col in range(cols):
            piece = part[spot, pl.ds(col, share, stride=cols), :]
            table = pl.ds(col * LANES, LANES)
            total = total + dot3(piece, gh_ref[table, :], gl_ref[table, :])
        out_ref[turn] = total * scale

    def end_phase():
        if ends:
            @pl.when(inner)
            def _():
                end_station = ((here - 1) // (chain - 3)) * (chain - 1)
                transform(end_arrived.at[0], 0, end_spectra, end_weighted, end_station)
                pass_left.wait()
                transform(end_arrived.at[2], 2, end_spectra, None, end_station)
                pass_right.wait()
                transform(end_arrived.at[1], 1, end_spectra, None, end_station)

            @pl.when(at_end)
            def _():
                to_inner.wait_send()

    compute(0)

    def turn_body(turn, carry):
        @pl.when(turn < rounds - 1)
        def _():
            compute(turn + 1)

        pass_near(turn)

        @pl.when(turn > 0)
        def _():
            pass_far(turn - 1)

            @pl.when(turn == 1)
            def _():
                end_phase()

            final(turn - 1)

        return carry

    lax.fori_loop(0, rounds, turn_body, 0)
    pass_far(rounds - 1)
    final(rounds - 1)

    def drain(turn, carry):
        for dest in range(chain):
            sent_up = (dest > here) & (here > 0) if by_end(True, dest) else dest > here
            sent_down = (dest < here) & (here < chain - 1) if by_end(False, dest) else dest < here

            @pl.when(sent_up)
            def _():
                upward(turn, dest).wait_send()

            @pl.when(sent_down)
            def _():
                downward(turn, dest).wait_send()
        return carry

    lax.fori_loop(0, rounds, drain, 0)


def on_device(waveforms, event_mask, station_weight, partners, pair_list, counts):
    events, stations, channels, samples = waveforms.shape
    rounds, _, pairs, _ = pair_list.shape
    ring = lax.axis_size("cluster")
    chain = lax.axis_size("station")
    rows = stations * channels
    share = pairs // chain
    cols = 2 * samples // LANES
    fh, fl, gh, gl = make_tables(samples)

    energy = jnp.sum(waveforms * waveforms, axis=-1, keepdims=True)
    unit = waveforms * (lax.rsqrt(energy + epsilon) * event_mask[:, :, None, None].astype(jnp.float32))
    traces = jnp.transpose(unit, (1, 2, 0, 3)).reshape(rows * events, samples)

    vmem = pl.BlockSpec(memory_space=pltpu.VMEM)
    smem = pl.BlockSpec(memory_space=pltpu.SMEM)
    hbm = pl.BlockSpec(memory_space=pltpu.HBM)
    lines = pltpu.VMEM((events, rows * cols, LANES), jnp.float32)
    all_lines = pltpu.VMEM((3 * events + 1, rows * cols, LANES), jnp.float32)
    blocks = rounds * chain
    block = pltpu.VMEM((blocks, share * cols, LANES), jnp.float32)
    out = pl.pallas_call(
        functools.partial(kernel, (events, rows, rounds, chain, share, ring, channels)),
        out_shape=jax.ShapeDtypeStruct((rounds, share, 2 * samples), jnp.float32),
        in_specs=[smem] * 4 + [vmem] + [hbm] * 4,
        out_specs=vmem,
        scratch_shapes=[
            *(pltpu.VMEM(table.shape, jnp.bfloat16) for table in (fh, fl, gh, gl)),
            pltpu.VMEM((2, rows * events, samples), jnp.float32),
            pltpu.VMEM((3, rows * events, samples), jnp.float32),
            lines, all_lines, lines, all_lines,
            block, block, block,
            pltpu.SemaphoreType.DMA((4,)),
            pltpu.SemaphoreType.DMA((2,)), pltpu.SemaphoreType.DMA((2,)),
            pltpu.SemaphoreType.DMA((3,)), pltpu.SemaphoreType.DMA((3,)),
            pltpu.SemaphoreType.DMA((blocks,)), pltpu.SemaphoreType.DMA((blocks,)),
            pltpu.SemaphoreType.DMA((blocks,)), pltpu.SemaphoreType.DMA((blocks,)),
        ],
        compiler_params=pltpu.CompilerParams(
            collective_id=0, has_side_effects=True, vmem_limit_bytes=48 << 20),
        name="stack_pairs",
    )(pair_list.reshape(-1), partners.reshape(-1), counts, station_weight, traces, fh, fl, gh, gl)
    return out[:, None]


def solution(mesh):
    return jax.shard_map(
        on_device,
        mesh=mesh,
        in_specs=(
            P(("groups", "cluster"), "station", None, None),
            P(("groups", "cluster"), "station"),
            P("groups"),
            P(None, "groups"),
            P(None, ("groups", "cluster"), None, None),
            P("groups"),
        ),
        out_specs=P(None, ("groups", "cluster"), "station", None),
        check_vma=False,
    )
```

```python
import functools
import math

import jax
import jax.numpy as jnp
import numpy as np
from jax import lax
from jax.experimental import pallas as pl
from jax.experimental.pallas import tpu as pltpu
from jax.sharding import PartitionSpec as P

epsilon = 1e-06
LANES = 128
MESH = pl.DeviceIdType.MESH


def split_table(table):
    high = table.astype(np.float32).astype(jnp.bfloat16)
    low = (table - high.astype(np.float64)).astype(np.float32).astype(jnp.bfloat16)
    return np.asarray(high), np.asarray(low)


def make_tables(samples):
    duration = 2 * samples
    time_points = np.arange(samples)
    angles = (time_points[:, None] * time_points[None, :] % duration) * (math.pi / samples)
    forward = np.concatenate([np.cos(angles), -np.sin(angles)], axis=1)
    lags = (np.arange(duration) + samples) % duration
    back = (time_points[:, None] * lags[None, :] % duration) * (math.pi / samples)
    scale = np.where(time_points == 0, 1.0, 2.0)[:, None] / duration
    inverse = np.concatenate([scale * np.cos(back), -scale * np.sin(back)], axis=0)
    return split_table(forward) + split_table(inverse)


def halves(x):
    high = x.astype(jnp.bfloat16)
    return high, (x - high.astype(jnp.float32)).astype(jnp.bfloat16)


def dot3(x, table_high, table_low):
    high, low = halves(x)
    dot = functools.partial(jnp.dot, preferred_element_type=jnp.float32)
    return dot(high, table_high) + (dot(high, table_low) + dot(low, table_high))


def kernel(sizes, pair_ref, partner_ref, count_ref, weight_ref, traces_ref, fh_hbm, fl_hbm, gh_hbm,
           gl_hbm, out_ref, fh_ref, fl_ref, gh_ref, gl_ref, arrived, end_arrived, weighted,
           spectra, end_weighted, end_spectra, part, from_below, from_above, table_sem, side_send,
           side_recv, end_send, end_recv, up_send, up_recv, down_send, down_recv):
    events, rows, rounds, chain, share, ring, channels = sizes
    cols = fh_ref.shape[1] // LANES
    half = cols // 2
    lines = rows * cols
    cluster = lax.axis_index("cluster")
    here = lax.axis_index("station")
    right, left = lax.rem(cluster + 1, ring), lax.rem(cluster + ring - 1, ring)

    tables = [
        pltpu.make_async_copy(source, target, table_sem.at[k])
        for k, (source, target) in enumerate(
            ((fh_hbm, fh_ref), (fl_hbm, fl_ref), (gh_hbm, gh_ref), (gl_hbm, gl_ref)))
    ]
    for table in tables:
        table.start()

    barrier = pltpu.get_barrier_semaphore()
    for side in (left, right):
        pl.semaphore_signal(barrier, inc=1, device_id={"cluster": side}, device_id_type=MESH)

    @pl.when(here > 0)
    def _():
        pl.semaphore_signal(barrier, inc=1, device_id={"station": here - 1}, device_id_type=MESH)

    @pl.when(here < chain - 1)
    def _():
        pl.semaphore_signal(barrier, inc=1, device_id={"station": here + 1}, device_id_type=MESH)

    pl.semaphore_wait(barrier, 2 + (here + chain - 1) // chain + (2 * chain - 2 - here) // chain)

    def to_side(slot, side):
        return pltpu.make_async_remote_copy(
            src_ref=traces_ref, dst_ref=arrived.at[slot], send_sem=side_send.at[slot],
            recv_sem=side_recv.at[slot], device_id={"cluster": side}, device_id_type=MESH)

    to_right, to_left = to_side(0, right), to_side(1, left)
    to_right.start()
    to_left.start()

    ends = chain >= 4
    pitch = chain - 1 if ends else 1
    at_end = (here == 0) | (here == chain - 1)
    inner = (here == 1) | (here == chain - 2)
    inward = 1 + (here // pitch) * (chain - 3) if ends else here

    def end_copy(k, source, where):
        return pltpu.make_async_remote_copy(
            src_ref=source, dst_ref=end_arrived.at[k], send_sem=end_send.at[k],
            recv_sem=end_recv.at[k], device_id=where, device_id_type=MESH)

    to_inner = end_copy(0, traces_ref, {"station": inward})
    pass_right = end_copy(1, end_arrived.at[0], {"cluster": right})
    pass_left = end_copy(2, end_arrived.at[0], {"cluster": left})

    if ends:
        @pl.when(at_end)
        def _():
            to_inner.start()

    def place(values, row, base, ref):
        for col in range(cols):
            line = (col // half) * (lines // 2) + row * half + col % half
            start = base * lines + line
            flat = ref.reshape(ref.shape[0] * lines, LANES)
            flat[pl.ds(start, events, stride=lines), :] = values[:, col * LANES:(col + 1) * LANES]

    def transform(source, slot, spectra_to, weighted_to, station):
        group = 4 if rows % 4 == 0 else 1
        for first in range(0, rows, group):
            found = source[pl.ds(first * events, group * events), :]
            found = found * lax.rsqrt(jnp.sum(found * found, axis=-1, keepdims=True) + epsilon)
            found = dot3(found, fh_ref[...], fl_ref[...])
            for k in range(group):
                row = first + k
                values = found[k * events:(k + 1) * events]
                place(values, row, slot * events, spectra_to)
                if weighted_to is not None:
                    weight = weight_ref[station * (rows // channels) + row // channels]
                    place(values * weight, row, 0, weighted_to)

    spectra[3 * events] = jnp.zeros(spectra.shape[1:], jnp.float32)
    end_spectra[3 * events] = jnp.zeros(spectra.shape[1:], jnp.float32)
    tables[0].wait()
    tables[1].wait()
    transform(traces_ref, 0, spectra, weighted, here)
    to_left.wait()
    transform(arrived.at[1], 2, spectra, None, here)
    to_right.wait()
    if ends:
        @pl.when(inner)
        def _():
            to_inner.wait_recv()
            pass_right.start()
            pass_left.start()

    transform(arrived.at[0], 1, spectra, None, here)
    tables[2].wait()
    tables[3].wait()

    sub = lax.broadcasted_iota(jnp.int32, (8, LANES), 0)
    in_low4 = sub < 4
    in_low2 = (sub & 2) == 0

    def fold(x, y, lower, by):
        return jnp.where(lower, x, y) + pltpu.roll(jnp.where(lower, y, x), by, 0)

    deep = lines // 2

    def one_pair(spot, turn_facts, left_rows, right_rows):
        slot, own_count, other_count = turn_facts
        first, second = pair_ref[2 * spot], pair_ref[2 * spot + 1]
        valid = (first < own_count) & (second < other_count)
        a = left_rows[first]
        b = right_rows[jnp.where(valid, slot * events + second, 3 * events)]
        re_a, im_a, re_b, im_b = a[:deep], a[deep:], b[:deep], b[deep:]
        real = re_a * re_b + im_a * im_b
        imag = im_a * re_b - re_a * im_b
        return (sum(real[k:k + 8] for k in range(0, deep, 8)),
                sum(imag[k:k + 8] for k in range(0, deep, 8)))

    def fill(turn, dest, left_rows, right_rows, add):
        base = (turn * chain + dest) * share
        partner = partner_ref[turn, cluster]
        slot = jnp.where(partner == cluster, 0, jnp.where(partner == right, 2, 1))
        turn_facts = (slot, count_ref[cluster], count_ref[partner])

        def body(step, carry):
            for k in range(0, 8, 2):
                spot = base + step * 8 + k
                real0, imag0 = one_pair(spot, turn_facts, left_rows, right_rows)
                real1, imag1 = one_pair(spot + 1, turn_facts, left_rows, right_rows)
                reals = fold(real0, real1, in_low4, 4)
                imags = fold(imag0, imag1, in_low4, 4)
                both = jnp.where(in_low2, reals, imags) + jnp.where(
                    in_low2, pltpu.roll(reals, 6, 0), pltpu.roll(imags, 2, 0))
                place_at = pl.ds(pl.multiple_of(step * 32 + k * 4, 8), 8)
                if add:
                    both = both + part[turn * chain + dest, place_at, :]
                part[turn * chain + dest, place_at, :] = both
            return carry

        lax.fori_loop(0, share // 8, body, 0)

    def upward(turn, dest):
        spot = turn * chain + dest
        return pltpu.make_async_remote_copy(
            src_ref=part.at[spot], dst_ref=from_below.at[spot], send_sem=up_send.at[spot],
            recv_sem=up_recv.at[spot], device_id={"station": here + 1}, device_id_type=MESH)

    def downward(turn, dest):
        spot = turn * chain + dest
        return pltpu.make_async_remote_copy(
            src_ref=part.at[spot], dst_ref=from_above.at[spot], send_sem=down_send.at[spot],
            recv_sem=down_recv.at[spot], device_id={"station": here - 1}, device_id_type=MESH)

    far_first = sorted(range(chain), key=lambda d: -abs(2 * d - chain + 1))

    def by_end(low, dest):
        if not ends:
            return False
        return dest == 1 if low else dest == chain - 2

    def compute(turn):
        for dest in far_first:
            given = ((here == 0) & by_end(True, dest)) | ((here == chain - 1) & by_end(False, dest))

            @pl.when(jnp.logical_not(given))
            def _():
                fill(turn, dest, weighted, spectra, False)

            if not by_end(True, dest):
                @pl.when((here == 0) & (dest > here))
                def _():
                    upward(turn, dest).start()

            if not by_end(False, dest):
                @pl.when((here == chain - 1) & (dest < here))
                def _():
                    downward(turn, dest).start()

    def pass_up(turn):
        for dest in far_first:
            spot = turn * chain + dest

            @pl.when((here > 0) & (dest > here))
            def _():
                upward(turn, dest).wait_recv()
                part[spot] = part[spot] + from_below[spot]
                upward(turn, dest).start()

    def pass_down(turn):
        for dest in far_first:
            spot = turn * chain + dest

            @pl.when((here < chain - 1) & (dest < here))
            def _():
                downward(turn, dest).wait_recv()
                part[spot] = part[spot] + from_above[spot]
                downward(turn, dest).start()

    lower = 2 * here < chain

    def pass_near(turn):
        @pl.when(lower)
        def _():
            pass_up(turn)

        @pl.when(jnp.logical_not(lower))
        def _():
            pass_down(turn)

    def pass_far(turn):
        @pl.when(lower)
        def _():
            pass_down(turn)

        @pl.when(jnp.logical_not(lower))
        def _():
            pass_up(turn)

    gets_below = (here > 1) if ends else (here > 0)
    gets_above = (here < chain - 2) if ends else (here < chain - 1)
    weight_sum = weight_ref[0]
    for k in range(1, weight_ref.shape[0]):
        weight_sum = weight_sum + weight_ref[k]
    scale = 1.0 / (channels * jnp.full((1, gh_ref.shape[1]), weight_sum, jnp.float32))

    def final(turn):
        spot = turn * chain + here

        if ends:
            @pl.when(inner)
            def _():
                fill(turn, here, end_weighted, end_spectra, True)

        @pl.when(gets_below)
        def _():
            upward(turn, here).wait_recv()
            part[spot] = part[spot] + from_below[spot]

        @pl.when(gets_above)
        def _():
            downward(turn, here).wait_recv()
            part[spot] = part[spot] + from_above[spot]

        total = jnp.zeros((share, gh_ref.shape[1]), jnp.float32)
        for col in range(cols):
            piece = part[spot, pl.ds(col, share, stride=cols), :]
            table = pl.ds(col * LANES, LANES)
            total = total + dot3(piece, gh_ref[table, :], gl_ref[table, :])
        out_ref[turn] = total * scale

    def end_phase():
        if ends:
            @pl.when(inner)
            def _():
                end_station = ((here - 1) // (chain - 3)) * (chain - 1)
                transform(end_arrived.at[0], 0, end_spectra, end_weighted, end_station)
                pass_left.wait()
                transform(end_arrived.at[2], 2, end_spectra, None, end_station)
                pass_right.wait()
                transform(end_arrived.at[1], 1, end_spectra, None, end_station)

            @pl.when(at_end)
            def _():
                to_inner.wait_send()

    compute(0)

    def turn_body(turn, carry):
        @pl.when(turn < rounds - 1)
        def _():
            compute(turn + 1)

        pass_near(turn)

        @pl.when(turn > 0)
        def _():
            pass_far(turn - 1)

            @pl.when(turn == 1)
            def _():
                end_phase()

            final(turn - 1)

        return carry

    lax.fori_loop(0, rounds, turn_body, 0)
    pass_far(rounds - 1)
    final(rounds - 1)

    def drain(turn, carry):
        for dest in range(chain):
            sent_up = (dest > here) & (here > 0) if by_end(True, dest) else dest > here
            sent_down = (dest < here) & (here < chain - 1) if by_end(False, dest) else dest < here

            @pl.when(sent_up)
            def _():
                upward(turn, dest).wait_send()

            @pl.when(sent_down)
            def _():
                downward(turn, dest).wait_send()
        return carry

    lax.fori_loop(0, rounds, drain, 0)


def on_device(waveforms, event_mask, station_weight, partners, pair_list, counts):
    events, stations, channels, samples = waveforms.shape
    rounds, _, pairs, _ = pair_list.shape
    ring = lax.axis_size("cluster")
    chain = lax.axis_size("station")
    rows = stations * channels
    share = pairs // chain
    cols = 2 * samples // LANES
    fh, fl, gh, gl = make_tables(samples)

    masked = waveforms * event_mask[:, :, None, None].astype(jnp.float32)
    traces = jnp.transpose(masked, (1, 2, 0, 3)).reshape(rows * events, samples)

    vmem = pl.BlockSpec(memory_space=pltpu.VMEM)
    smem = pl.BlockSpec(memory_space=pltpu.SMEM)
    hbm = pl.BlockSpec(memory_space=pltpu.HBM)
    lines = pltpu.VMEM((events, rows * cols, LANES), jnp.float32)
    all_lines = pltpu.VMEM((3 * events + 1, rows * cols, LANES), jnp.float32)
    blocks = rounds * chain
    block = pltpu.VMEM((blocks, share * cols, LANES), jnp.float32)
    out = pl.pallas_call(
        functools.partial(kernel, (events, rows, rounds, chain, share, ring, channels)),
        out_shape=jax.ShapeDtypeStruct((rounds, share, 2 * samples), jnp.float32),
        in_specs=[smem] * 4 + [vmem] + [hbm] * 4,
        out_specs=vmem,
        scratch_shapes=[
            *(pltpu.VMEM(table.shape, jnp.bfloat16) for table in (fh, fl, gh, gl)),
            pltpu.VMEM((2, rows * events, samples), jnp.float32),
            pltpu.VMEM((3, rows * events, samples), jnp.float32),
            lines, all_lines, lines, all_lines,
            block, block, block,
            pltpu.SemaphoreType.DMA((4,)),
            pltpu.SemaphoreType.DMA((2,)), pltpu.SemaphoreType.DMA((2,)),
            pltpu.SemaphoreType.DMA((3,)), pltpu.SemaphoreType.DMA((3,)),
            pltpu.SemaphoreType.DMA((blocks,)), pltpu.SemaphoreType.DMA((blocks,)),
            pltpu.SemaphoreType.DMA((blocks,)), pltpu.SemaphoreType.DMA((blocks,)),
        ],
        compiler_params=pltpu.CompilerParams(
            collective_id=0, has_side_effects=True, vmem_limit_bytes=48 << 20),
        name="stack_pairs",
    )(pair_list.reshape(-1), partners, counts, station_weight, traces, fh, fl, gh, gl)
    return out[:, None]


def solution(mesh):
    return jax.shard_map(
        on_device,
        mesh=mesh,
        in_specs=(
            P(("groups", "cluster"), "station", None, None),
            P(("groups", "cluster"), "station"),
            P("groups"),
            P(None, "groups"),
            P(None, ("groups", "cluster"), None, None),
            P("groups"),
        ),
        out_specs=P(None, ("groups", "cluster"), "station", None),
        check_vma=False,
    )
```

```python
import functools
import math

import jax
import jax.numpy as jnp
import numpy as np
from jax import lax
from jax.experimental import pallas as pl
from jax.experimental.pallas import tpu as pltpu
from jax.sharding import PartitionSpec as P

epsilon = 1e-06
LANES = 128
MESH = pl.DeviceIdType.MESH


def split_table(table):
    high = table.astype(np.float32).astype(jnp.bfloat16)
    low = (table - high.astype(np.float64)).astype(np.float32).astype(jnp.bfloat16)
    return np.asarray(high), np.asarray(low)


def make_tables(samples):
    duration = 2 * samples
    time_points = np.arange(samples)
    angles = (time_points[:, None] * time_points[None, :] % duration) * (math.pi / samples)
    forward = np.concatenate([np.cos(angles), -np.sin(angles)], axis=1)
    lags = (np.arange(duration) + samples) % duration
    back = (time_points[:, None] * lags[None, :] % duration) * (math.pi / samples)
    scale = np.where(time_points == 0, 1.0, 2.0)[:, None] / duration
    inverse = np.concatenate([scale * np.cos(back), -scale * np.sin(back)], axis=0)
    return split_table(forward) + split_table(inverse)


def halves(x):
    high = x.astype(jnp.bfloat16)
    return high, (x - high.astype(jnp.float32)).astype(jnp.bfloat16)


def dot3(x, table_high, table_low):
    high, low = halves(x)
    dot = functools.partial(jnp.dot, preferred_element_type=jnp.float32)
    return dot(high, table_high) + (dot(high, table_low) + dot(low, table_high))


def kernel(sizes, pair_ref, partner_ref, count_ref, weight_ref, traces_ref, fh_hbm, fl_hbm, gh_hbm,
           gl_hbm, out_ref, fh_ref, fl_ref, gh_ref, gl_ref, arrived, end_arrived, weighted,
           spectra, end_weighted, end_spectra, part, from_below, from_above, table_sem, side_send,
           side_recv, end_send, end_recv, up_send, up_recv, down_send, down_recv):
    events, rows, rounds, chain, share, ring, channels = sizes
    cols = fh_ref.shape[1] // LANES
    half = cols // 2
    lines = rows * cols
    cluster = lax.axis_index("cluster")
    here = lax.axis_index("station")
    right, left = lax.rem(cluster + 1, ring), lax.rem(cluster + ring - 1, ring)

    tables = [
        pltpu.make_async_copy(source, target, table_sem.at[k])
        for k, (source, target) in enumerate(
            ((fh_hbm, fh_ref), (fl_hbm, fl_ref), (gh_hbm, gh_ref), (gl_hbm, gl_ref)))
    ]
    for table in tables:
        table.start()

    barrier = pltpu.get_barrier_semaphore()
    for side in (left, right):
        pl.semaphore_signal(barrier, inc=1, device_id={"cluster": side}, device_id_type=MESH)

    @pl.when(here > 0)
    def _():
        pl.semaphore_signal(barrier, inc=1, device_id={"station": here - 1}, device_id_type=MESH)

    @pl.when(here < chain - 1)
    def _():
        pl.semaphore_signal(barrier, inc=1, device_id={"station": here + 1}, device_id_type=MESH)

    pl.semaphore_wait(barrier, 2 + (here + chain - 1) // chain + (2 * chain - 2 - here) // chain)

    def to_side(slot, side):
        return pltpu.make_async_remote_copy(
            src_ref=traces_ref, dst_ref=arrived.at[slot], send_sem=side_send.at[slot],
            recv_sem=side_recv.at[slot], device_id={"cluster": side}, device_id_type=MESH)

    to_right, to_left = to_side(0, right), to_side(1, left)
    to_right.start()
    to_left.start()

    ends = chain >= 4
    pitch = chain - 1 if ends else 1
    at_end = (here == 0) | (here == chain - 1)
    inner = (here == 1) | (here == chain - 2)
    inward = 1 + (here // pitch) * (chain - 3) if ends else here

    def end_copy(k, source, where):
        return pltpu.make_async_remote_copy(
            src_ref=source, dst_ref=end_arrived.at[k], send_sem=end_send.at[k],
            recv_sem=end_recv.at[k], device_id=where, device_id_type=MESH)

    to_inner = end_copy(0, traces_ref, {"station": inward})
    pass_right = end_copy(1, end_arrived.at[0], {"cluster": right})
    pass_left = end_copy(2, end_arrived.at[0], {"cluster": left})

    if ends:
        @pl.when(at_end)
        def _():
            to_inner.start()

    def place(values, row, base, ref):
        for col in range(cols):
            line = (col // half) * (lines // 2) + row * half + col % half
            start = base * lines + line
            flat = ref.reshape(ref.shape[0] * lines, LANES)
            flat[pl.ds(start, events, stride=lines), :] = values[:, col * LANES:(col + 1) * LANES]

    def transform(source, slot, spectra_to, weighted_to, station):
        group = 4 if rows % 4 == 0 else 1
        for first in range(0, rows, group):
            found = source[pl.ds(first * events, group * events), :]
            found = found * lax.rsqrt(jnp.sum(found * found, axis=-1, keepdims=True) + epsilon)
            found = dot3(found, fh_ref[...], fl_ref[...])
            for k in range(group):
                row = first + k
                values = found[k * events:(k + 1) * events]
                place(values, row, slot * events, spectra_to)
                if weighted_to is not None:
                    weight = weight_ref[station * (rows // channels) + row // channels]
                    place(values * weight, row, 0, weighted_to)

    spectra[3 * events] = jnp.zeros(spectra.shape[1:], jnp.float32)
    end_spectra[3 * events] = jnp.zeros(spectra.shape[1:], jnp.float32)
    tables[0].wait()
    tables[1].wait()
    transform(traces_ref, 0, spectra, weighted, here)
    to_left.wait()
    transform(arrived.at[1], 2, spectra, None, here)
    to_right.wait()
    if ends:
        @pl.when(inner)
        def _():
            to_inner.wait_recv()
            pass_right.start()
            pass_left.start()

    transform(arrived.at[0], 1, spectra, None, here)
    tables[2].wait()
    tables[3].wait()

    sub = lax.broadcasted_iota(jnp.int32, (8, LANES), 0)
    in_low4 = sub < 4
    in_low2 = (sub & 2) == 0

    def fold(x, y, lower, by):
        return jnp.where(lower, x, y) + pltpu.roll(jnp.where(lower, y, x), by, 0)

    deep = lines // 2

    def one_pair(spot, turn_facts, left_rows, right_rows):
        offset, slot, own_count, other_count = turn_facts
        first, second = pair_ref[spot + offset], pair_ref[spot + offset + chain * share]
        valid = (first < own_count) & (second < other_count)
        a = left_rows[first]
        b = right_rows[jnp.where(valid, slot * events + second, 3 * events)]
        re_a, im_a, re_b, im_b = a[:deep], a[deep:], b[:deep], b[deep:]
        real = re_a * re_b + im_a * im_b
        imag = im_a * re_b - re_a * im_b
        return (sum(real[k:k + 8] for k in range(0, deep, 8)),
                sum(imag[k:k + 8] for k in range(0, deep, 8)))

    def fill(turn, dest, left_rows, right_rows, add):
        base = (turn * chain + dest) * share
        partner = partner_ref[turn, cluster]
        slot = jnp.where(partner == cluster, 0, jnp.where(partner == right, 2, 1))
        turn_facts = (turn * chain * share, slot, count_ref[cluster], count_ref[partner])

        def body(step, carry):
            for k in range(0, 8, 2):
                spot = base + step * 8 + k
                real0, imag0 = one_pair(spot, turn_facts, left_rows, right_rows)
                real1, imag1 = one_pair(spot + 1, turn_facts, left_rows, right_rows)
                reals = fold(real0, real1, in_low4, 4)
                imags = fold(imag0, imag1, in_low4, 4)
                both = jnp.where(in_low2, reals, imags) + jnp.where(
                    in_low2, pltpu.roll(reals, 6, 0), pltpu.roll(imags, 2, 0))
                place_at = pl.ds(pl.multiple_of(step * 32 + k * 4, 8), 8)
                if add:
                    both = both + part[turn * chain + dest, place_at, :]
                part[turn * chain + dest, place_at, :] = both
            return carry

        lax.fori_loop(0, share // 8, body, 0)

    def upward(turn, dest):
        spot = turn * chain + dest
        return pltpu.make_async_remote_copy(
            src_ref=part.at[spot], dst_ref=from_below.at[spot], send_sem=up_send.at[spot],
            recv_sem=up_recv.at[spot], device_id={"station": here + 1}, device_id_type=MESH)

    def downward(turn, dest):
        spot = turn * chain + dest
        return pltpu.make_async_remote_copy(
            src_ref=part.at[spot], dst_ref=from_above.at[spot], send_sem=down_send.at[spot],
            recv_sem=down_recv.at[spot], device_id={"station": here - 1}, device_id_type=MESH)

    far_first = sorted(range(chain), key=lambda d: -abs(2 * d - chain + 1))

    def by_end(low, dest):
        if not ends:
            return False
        return dest == 1 if low else dest == chain - 2

    def compute(turn):
        for dest in far_first:
            given = ((here == 0) & by_end(True, dest)) | ((here == chain - 1) & by_end(False, dest))

            @pl.when(jnp.logical_not(given))
            def _():
                fill(turn, dest, weighted, spectra, False)

            if not by_end(True, dest):
                @pl.when((here == 0) & (dest > here))
                def _():
                    upward(turn, dest).start()

            if not by_end(False, dest):
                @pl.when((here == chain - 1) & (dest < here))
                def _():
                    downward(turn, dest).start()

    def pass_up(turn):
        for dest in far_first:
            spot = turn * chain + dest

            @pl.when((here > 0) & (dest > here))
            def _():
                upward(turn, dest).wait_recv()
                part[spot] = part[spot] + from_below[spot]
                upward(turn, dest).start()

    def pass_down(turn):
        for dest in far_first:
            spot = turn * chain + dest

            @pl.when((here < chain - 1) & (dest < here))
            def _():
                downward(turn, dest).wait_recv()
                part[spot] = part[spot] + from_above[spot]
                downward(turn, dest).start()

    lower = 2 * here < chain

    def pass_near(turn):
        @pl.when(lower)
        def _():
            pass_up(turn)

        @pl.when(jnp.logical_not(lower))
        def _():
            pass_down(turn)

    def pass_far(turn):
        @pl.when(lower)
        def _():
            pass_down(turn)

        @pl.when(jnp.logical_not(lower))
        def _():
            pass_up(turn)

    gets_below = (here > 1) if ends else (here > 0)
    gets_above = (here < chain - 2) if ends else (here < chain - 1)
    weight_sum = weight_ref[0]
    for k in range(1, weight_ref.shape[0]):
        weight_sum = weight_sum + weight_ref[k]
    scale = 1.0 / (channels * jnp.full((1, gh_ref.shape[1]), weight_sum, jnp.float32))

    def final(turn):
        spot = turn * chain + here

        if ends:
            @pl.when(inner)
            def _():
                fill(turn, here, end_weighted, end_spectra, True)

        @pl.when(gets_below)
        def _():
            upward(turn, here).wait_recv()
            part[spot] = part[spot] + from_below[spot]

        @pl.when(gets_above)
        def _():
            downward(turn, here).wait_recv()
            part[spot] = part[spot] + from_above[spot]

        total = jnp.zeros((share, gh_ref.shape[1]), jnp.float32)
        for col in range(cols):
            piece = part[spot, pl.ds(col, share, stride=cols), :]
            table = pl.ds(col * LANES, LANES)
            total = total + dot3(piece, gh_ref[table, :], gl_ref[table, :])
        out_ref[turn] = total * scale

    def end_phase():
        if ends:
            @pl.when(inner)
            def _():
                end_station = ((here - 1) // (chain - 3)) * (chain - 1)
                transform(end_arrived.at[0], 0, end_spectra, end_weighted, end_station)
                pass_left.wait()
                transform(end_arrived.at[2], 2, end_spectra, None, end_station)
                pass_right.wait()
                transform(end_arrived.at[1], 1, end_spectra, None, end_station)

            @pl.when(at_end)
            def _():
                to_inner.wait_send()

    compute(0)

    def turn_body(turn, carry):
        @pl.when(turn < rounds - 1)
        def _():
            compute(turn + 1)

        pass_near(turn)

        @pl.when(turn > 0)
        def _():
            pass_far(turn - 1)

            @pl.when(turn == 1)
            def _():
                end_phase()

            final(turn - 1)

        return carry

    lax.fori_loop(0, rounds, turn_body, 0)
    pass_far(rounds - 1)
    final(rounds - 1)

    def drain(turn, carry):
        for dest in range(chain):
            sent_up = (dest > here) & (here > 0) if by_end(True, dest) else dest > here
            sent_down = (dest < here) & (here < chain - 1) if by_end(False, dest) else dest < here

            @pl.when(sent_up)
            def _():
                upward(turn, dest).wait_send()

            @pl.when(sent_down)
            def _():
                downward(turn, dest).wait_send()
        return carry

    lax.fori_loop(0, rounds, drain, 0)


def on_device(waveforms, event_mask, station_weight, partners, pair_list, counts):
    events, stations, channels, samples = waveforms.shape
    rounds, _, pairs, _ = pair_list.shape
    ring = lax.axis_size("cluster")
    chain = lax.axis_size("station")
    rows = stations * channels
    share = pairs // chain
    cols = 2 * samples // LANES
    fh, fl, gh, gl = make_tables(samples)

    masked = waveforms * event_mask[:, :, None, None].astype(jnp.float32)
    traces = jnp.transpose(masked, (1, 2, 0, 3)).reshape(rows * events, samples)

    vmem = pl.BlockSpec(memory_space=pltpu.VMEM)
    smem = pl.BlockSpec(memory_space=pltpu.SMEM)
    hbm = pl.BlockSpec(memory_space=pltpu.HBM)
    lines = pltpu.VMEM((events, rows * cols, LANES), jnp.float32)
    all_lines = pltpu.VMEM((3 * events + 1, rows * cols, LANES), jnp.float32)
    blocks = rounds * chain
    block = pltpu.VMEM((blocks, share * cols, LANES), jnp.float32)
    out = pl.pallas_call(
        functools.partial(kernel, (events, rows, rounds, chain, share, ring, channels)),
        out_shape=jax.ShapeDtypeStruct((rounds, share, 2 * samples), jnp.float32),
        in_specs=[smem] * 4 + [vmem] + [hbm] * 4,
        out_specs=vmem,
        scratch_shapes=[
            *(pltpu.VMEM(table.shape, jnp.bfloat16) for table in (fh, fl, gh, gl)),
            pltpu.VMEM((2, rows * events, samples), jnp.float32),
            pltpu.VMEM((3, rows * events, samples), jnp.float32),
            lines, all_lines, lines, all_lines,
            block, block, block,
            pltpu.SemaphoreType.DMA((4,)),
            pltpu.SemaphoreType.DMA((2,)), pltpu.SemaphoreType.DMA((2,)),
            pltpu.SemaphoreType.DMA((3,)), pltpu.SemaphoreType.DMA((3,)),
            pltpu.SemaphoreType.DMA((blocks,)), pltpu.SemaphoreType.DMA((blocks,)),
            pltpu.SemaphoreType.DMA((blocks,)), pltpu.SemaphoreType.DMA((blocks,)),
        ],
        compiler_params=pltpu.CompilerParams(
            collective_id=0, has_side_effects=True, vmem_limit_bytes=48 << 20),
        name="stack_pairs",
    )(jnp.transpose(pair_list, (0, 1, 3, 2)).reshape(-1), partners, counts, station_weight, traces, fh, fl, gh, gl)
    return out[:, None]


def solution(mesh):
    return jax.shard_map(
        on_device,
        mesh=mesh,
        in_specs=(
            P(("groups", "cluster"), "station", None, None),
            P(("groups", "cluster"), "station"),
            P("groups"),
            P(None, "groups"),
            P(None, ("groups", "cluster"), None, None),
            P("groups"),
        ),
        out_specs=P(None, ("groups", "cluster"), "station", None),
        check_vma=False,
    )
```
